32 devices in a mesh: tx: 2 (over x), ty: 4 (over z), pg: 4 (over y, core).
Axes of the slice: x: 2, y: 2, z: 4, core: 2. Of those that a mesh axis runs over, the one named last changes fastest.
Arguments:
- direct_modes: bfloat16 [64, 3, 32, 512], P('pg', None, 'tx', 'ty'), may hold values from -6 to 6
- adjoint_modes: bfloat16 [64, 3, 32, 512], P(None, None, 'tx', 'ty'), may hold values from -6 to 6
- block_order: int32 [8], replicated, may hold values from 0 to 7, each once
Outputs:
- tensor: float32 [64, 64, 64], P('pg', 'ty', 'tx')
The draws below stay inside these ranges and needn't reach their ends.
Inputs may be any that keep to these rules, and one draw needn't show every extreme that they name: `block_order`: each of the 8 blocks appears exactly once.
All inputs are finite; a program needn't handle non-finite values.
Results may differ from the reference program's by a relative error of at most 0.0043.
Values may be sent and summed in bfloat16 or wider, within the bound.
A program may use at most 64 MiB of HBM per device.

```python
import math
import jax
import jax.numpy as jnp
from jax import lax

R = 64
K = 64
NBLK = 8
JB = 4
CZ = 4
NX = 32
NY = 128


def block_scale(key, shape, cuts, low, largest):
    def one(axis_at, shards_of):
        heights = jax.random.uniform(jax.random.fold_in(jax.random.fold_in(key, 6), axis_at), (shards_of,), jnp.float32, low / len(cuts), largest / len(cuts))
        return jnp.repeat(jnp.exp(heights), shape[axis_at] // shards_of).reshape((-1,) + (1,) * (len(shape) - axis_at - 1))

    loudness = one(*cuts[0])
    for cut in cuts[1:]:
        loudness = loudness * one(*cut)
    return loudness


def scatter_about(stream_key, shape, scale, reach, cuts=(), held_as=jnp.bfloat16):
    entries = scale * jax.random.normal(stream_key, shape, jnp.float32)
    if cuts:
        entries = entries * block_scale(stream_key, shape, cuts, -0.22, 0.18)
    return jnp.clip(entries, -reach, reach).astype(held_as)


def setup_inputs(seed: int = 0) -> dict:
    splits = jax.random.split(jax.random.key(seed), 4)
    return {
        "direct_modes": scatter_about(splits[0], (R, 3, NX, NY * CZ), 1.0, 6.0, ((0, 4), (2, 2), (3, 4))),
        "adjoint_modes": scatter_about(splits[1], (K, 3, NX, NY * CZ), 1.0, 6.0, ((2, 2), (3, 4))),
        "block_order": jax.random.permutation(splits[2], NBLK).astype(jnp.int32),
    }


def depth_slope(values, depth):
    position = jnp.arange(values.shape[-1]) % depth
    upper = jnp.where(position == depth - 1, jnp.roll(values, depth - 1, -1), jnp.roll(values, -1, -1))
    lower = jnp.where(position == 0, jnp.roll(values, 1 - depth, -1), jnp.roll(values, 1, -1))
    return (upper - lower) * 0.5

def slopes(values, wide_x, wide_y, depth):
    along_x = (wide_x[:, :, 2:] - wide_x[:, :, :-2]) * 0.5
    along_y = (wide_y[..., 2 * depth:] - wide_y[..., :-2 * depth]) * 0.5
    along_z = depth_slope(values, depth)
    return jnp.stack([along_x, along_y, along_z], 1).astype(jnp.bfloat16)

def pair_terms(rows_u, rows_g, cols_u, cols_g):
    result = jnp.zeros((rows_u.shape[0], cols_u.shape[0]) + cols_g.shape[2:], jnp.float32)
    for direction in range(3):
        result = result + rows_u[:, None, direction, None] * cols_g[None, :, direction]
        result = result + cols_u[None, :, direction, None] * rows_g[:, None, direction]
    return result.astype(jnp.bfloat16)

def project(pairs, adjoint):
    flat = pairs.reshape(pairs.shape[0] * pairs.shape[1], -1)
    basis = adjoint.reshape(adjoint.shape[0], -1)
    product = lax.dot_general(flat, basis, (((1,), (1,)), ((), ())), preferred_element_type=jnp.float32)
    return product.reshape(pairs.shape[0], pairs.shape[1], adjoint.shape[0])

def block_tensor(rows_u, rows_g, modes, grads, adjoint, width):
    count = modes.shape[0] // width

    def one_block(start):
        cols_u = lax.dynamic_slice_in_dim(modes, start, width, 0).astype(jnp.float32)
        cols_g = lax.dynamic_slice_in_dim(grads, start, width, 0).astype(jnp.float32)
        return project(pair_terms(rows_u, rows_g, cols_u, cols_g), adjoint)
    starts = (jnp.arange(count) * width).astype(jnp.int32)
    pieces = lax.map(one_block, starts)
    return jnp.transpose(pieces, (1, 0, 2, 3)).reshape(rows_u.shape[0], modes.shape[0], adjoint.shape[0])

def reference(direct_modes, adjoint_modes, block_order):
    values = direct_modes.astype(jnp.float32)
    wide_x = jnp.pad(values, ((0, 0), (0, 0), (1, 1), (0, 0)))
    wide_y = jnp.pad(values, ((0, 0), (0, 0), (0, 0), (CZ, CZ)))
    grads = slopes(values, wide_x, wide_y, CZ)
    block_rows = R // NBLK
    weight = 1.0 / math.sqrt(3.0 * NX * NY * CZ)

    def one_slot(block):
        start = (block * block_rows).astype(jnp.int32)
        rows_u = lax.dynamic_slice_in_dim(direct_modes, start, block_rows, 0).astype(jnp.float32)
        rows_g = lax.dynamic_slice_in_dim(grads, start, block_rows, 0).astype(jnp.float32)
        return block_tensor(rows_u, rows_g, direct_modes, grads, adjoint_modes, JB) * weight
    slots = lax.map(one_slot, block_order)
    return slots.reshape(R, R, K)
```

```python
import functools
import math

import jax
import jax.numpy as jnp
from jax import lax
from jax.experimental import pallas as pl
from jax.experimental.pallas import tpu as pltpu
from jax.sharding import PartitionSpec as P

NBLK = 8
CZ = 4
MESH = pl.DeviceIdType.MESH
F32 = jnp.float32
BF16 = jnp.bfloat16
WORK = BF16


def kernel(
    tx_n, ty_n, pg_n, weight,
    order_ref, own_any, adj_any, out_ref,
    own_in, own_sem, own_flat, own_ref, adj_raw, adj_flat, adj_sem, wide, face, edge, col_u, col_g, row_u, row_g,
    acc, sib_in, stage, parts, mine,
    mode_send, mode_recv, x_send, x_recv, y_send, y_recv, sib_send, sib_recv, part_send, part_recv,
):
    tx, ty, pg = lax.axis_index("tx"), lax.axis_index("ty"), lax.axis_index("pg")
    nx, _, own_n, lanes = own_ref.shape
    adj_n = adj_raw.shape[0]
    half = nx // 2
    steps = half // 2
    blk = pg_n * own_n // NBLK
    per_pair = 2 * NBLK // pg_n
    per_own = per_pair // 2
    co, hi = lax.rem(pg, 2), pg // 2
    sib = pg + 1 - 2 * co
    group_n = tx_n * ty_n
    me = tx * ty_n + ty

    own_copy = pltpu.make_async_copy(own_any, own_in, own_sem)
    own_copy.start()
    adj_copy = pltpu.make_async_copy(adj_any, adj_raw, adj_sem)
    adj_copy.start()

    has_xl, has_xh = tx > 0, tx < tx_n - 1
    has_yl, has_yh = ty > 0, ty < ty_n - 1

    barrier = pltpu.get_barrier_semaphore()
    for off in range(1, pg_n):
        pl.semaphore_signal(barrier, inc=1, device_id=(tx, ty, lax.rem(pg + off, pg_n)), device_id_type=MESH)
    for off in range(1, group_n):
        to = lax.rem(me + off, group_n)
        pl.semaphore_signal(barrier, inc=1, device_id=(to // ty_n, lax.rem(to, ty_n), pg), device_id_type=MESH)
    for has, dx, dy in ((has_xl, -1, 0), (has_xh, 1, 0), (has_yl, 0, -1), (has_yh, 0, 1)):
        @pl.when(has)
        def _():
            for off in range(1, pg_n):
                pl.semaphore_signal(
                    barrier, inc=1, device_id=(tx + dx, ty + dy, lax.rem(pg + off, pg_n)), device_id_type=MESH)

    own_copy.wait()
    for m in range(own_n):
        for c in range(3):
            own_flat[pl.ds(c * own_n + m, nx, stride=3 * own_n), :] = own_in[m, c].astype(F32)
    for x in range(nx):
        for c in range(3):
            own_ref[x, c] = own_flat[pl.ds((x * 3 + c) * own_n, own_n), :].astype(BF16)

    neighbours = (has_xl.astype(jnp.int32) + has_xh.astype(jnp.int32)
                  + has_yl.astype(jnp.int32) + has_yh.astype(jnp.int32))
    pl.semaphore_wait(barrier, (pg_n - 1) + (group_n - 1) + neighbours * (pg_n - 1))

    def span(t):
        return (0 if t == 0 else 2 + 2 * t), min(4 + 2 * t, half + 1)

    def mode_copy(off, t, src_pg, dst_pg):
        first, last = span(t)
        q = lax.rem(dst_pg, 2)
        at = q * first + (1 - q) * (half + 2 - last)
        return pltpu.make_async_remote_copy(
            own_ref.at[pl.ds(at + q * half - 1, last - first)], wide.at[pl.ds(at, last - first), src_pg],
            mode_send.at[off, t], mode_recv.at[off, t], device_id=(tx, ty, dst_pg), device_id_type=MESH)

    def mode_out(off, t):
        return mode_copy(off, t, pg, lax.rem(pg + off, pg_n))

    def mode_in(off, t):
        return mode_copy(off, t, lax.rem(pg + pg_n - off, pg_n), pg)

    def x_out(side, h):
        src, at, to = (nx - 1, 0, tx + 1) if side == 0 else (0, half + 1, tx - 1)
        return pltpu.make_async_remote_copy(
            own_ref.at[src], wide.at[at, pg], x_send.at[side, h], x_recv.at[pg],
            device_id=(to, ty, 2 * h + side), device_id_type=MESH)

    def x_in(source):
        return pltpu.make_async_remote_copy(
            own_ref.at[0], wide.at[co * (half + 1), source], x_send.at[0, 0], x_recv.at[source],
            device_id=(tx, ty, pg), device_id_type=MESH)

    def y_out(side, d):
        return pltpu.make_async_remote_copy(
            face.at[side, d % 2], edge.at[side, pg], y_send.at[side, d], y_recv.at[side, pg],
            device_id=(tx, ty + 1 - 2 * side, d), device_id_type=MESH)

    def y_in(side, source):
        return pltpu.make_async_remote_copy(
            face.at[side, 0], edge.at[side, source], y_send.at[side, 0], y_recv.at[side, source],
            device_id=(tx, ty, pg), device_id_type=MESH)

    y_sides = ((0, has_yh, has_yl), (1, has_yl, has_yh))
    x_sides = ((0, has_xh), (1, has_xl))
    gets_x = jnp.logical_or(jnp.logical_and(co == 0, has_xl), jnp.logical_and(co == 1, has_xh))
    far_first = [off for off in range(1, pg_n)]

    for off in far_first:
        mode_out(off, 0).start()

    lane = lax.broadcasted_iota(jnp.int32, (own_n, lanes), 1)
    for side in range(2):
        for q in range(2):
            packed = jnp.zeros((own_n, lanes), F32)
            for c in range(3):
                for i in range(half):
                    tile = own_ref[q * half + i, c].astype(F32)
                    at = (c * half + i) * CZ
                    shift = (at + (CZ if side == 0 else 0)) % lanes
                    here = (lane >= at) & (lane < at + CZ)
                    packed = jnp.where(here, pltpu.roll(tile, shift, 1) if shift else tile, packed)
            face[side, q] = packed.astype(BF16)
    for side, sends, _ in y_sides:
        @pl.when(sends)
        def _():
            for d in range(pg_n):
                y_out(side, d).start()
    for t in range(1, steps):
        for off in far_first:
            mode_out(off, t).start()
    for side, sends in x_sides:
        @pl.when(sends)
        def _():
            for h in range(pg_n // 2):
                x_out(side, h).start()

    wide[pl.ds(1 - co, half + 1), pg] = own_ref[pl.ds(co * (half - 1), half + 1)]

    @pl.when(jnp.logical_not(gets_x))
    def _():
        wide[co * (half + 1)] = jnp.zeros((pg_n, 3, own_n, lanes), BF16)

    for side, _, gets in y_sides:
        @pl.when(jnp.logical_not(gets))
        def _():
            edge[side] = jnp.zeros((pg_n, own_n, lanes), BF16)

    adj_copy.wait()

    def turn_basis(i, carry):
        for more in range(4):
            k = i * 4 + more
            for c in range(3):
                both = adj_raw[k, c].astype(F32)
                adj_flat[pl.ds(c * half * adj_n + k, half, stride=adj_n), :] = jnp.where(
                    co == 0, both[:half], both[half:])
        return carry

    lax.fori_loop(0, adj_n // 4, turn_basis, 0)

    for side, _, gets in y_sides:
        @pl.when(gets)
        def _():
            for p in range(pg_n):
                y_in(side, p).wait_recv()

    place = lax.rem(lane, CZ)
    tiles = own_n // blk

    def first_of(t):
        return co * (1 + 2 * t) + (1 - co) * (half - 1 - 2 * t)

    def grads(t):
        at = first_of(t)
        for xx in range(2):
            i, to = at + xx, 2 * t + xx
            for p in range(pg_n):
                for c in range(3):
                    u = wide[i, p, c].astype(F32)
                    col_u[to, c, pl.ds(p * tiles, tiles)] = u.reshape(tiles, blk, lanes)
                    gx = wide[i + 1, p, c].astype(F32) - wide[i - 1, p, c].astype(F32)
                    place_at = (c * half + i - 1) * CZ
                    e_hi = pltpu.roll(edge[1, p].astype(F32), lanes - CZ - place_at, 1)
                    e_lo = pltpu.roll(edge[0, p].astype(F32), lax.rem(lanes - place_at, lanes), 1)
                    up = jnp.where(lane >= lanes - CZ, e_hi, pltpu.roll(u, lanes - CZ, 1))
                    down = jnp.where(lane < CZ, e_lo, pltpu.roll(u, CZ, 1))
                    gy = up - down
                    upper = jnp.where(place == CZ - 1, pltpu.roll(u, CZ - 1, 1), pltpu.roll(u, lanes - 1, 1))
                    lower = jnp.where(place == 0, pltpu.roll(u, lanes - CZ + 1, 1), pltpu.roll(u, 1, 1))
                    gz = upper - lower
                    for d, g in enumerate((gx, gy, gz)):
                        g = (g * 0.5).astype(BF16).astype(F32)
                        col_g[to, d * 3 + c, pl.ds(p * tiles, tiles)] = g.reshape(tiles, blk, lanes)
            for h in range(2):
                group = lax.rem(co + 1 + h, 2)
                slots = [order_ref[hi * per_pair + group * per_own + b] for b in range(per_own)]
                for d in range(3):
                    row_u[to, d, h] = jnp.concatenate([col_u[to, d, s] for s in slots], 0).astype(WORK)
                for k in range(9):
                    row_g[to, k, h] = jnp.concatenate([col_g[to, k, s] for s in slots], 0).astype(WORK)

    chunk_j = own_n
    chunks = pg_n * own_n // chunk_j
    per_chunk = ty_n // chunks
    _, _, k_width, width = stage.shape
    units = chunks * steps

    def tensor(t, ch):
        at = first_of(t)
        made = None
        for c in range(3):
            halves = [[], []]
            for jj in range(chunk_j):
                jb, jr = ch * (chunk_j // blk) + jj // blk, pl.ds(jj % blk, 1)
                cells = [[], []]
                for xx in range(2):
                    x = 2 * t + xx
                    ju = [jnp.broadcast_to(col_u[x, d, jb, jr], (own_n, lanes)).astype(WORK) for d in range(3)]
                    jg = [jnp.broadcast_to(col_g[x, d * 3 + c, jb, jr], (own_n, lanes)).astype(WORK)
                          for d in range(3)]
                    for h in range(2):
                        v = [jg[d] * row_u[x, d, h] for d in range(3)]
                        v += [ju[d] * row_g[x, d * 3 + c, h] for d in range(3)]
                        total = ((v[0] + v[3]) + (v[1] + v[4])) + (v[2] + v[5])
                        cells[h].append(total.astype(BF16))
                for h in range(2):
                    halves[h].append(jnp.concatenate(cells[h], 1))
            basis = jnp.concatenate(
                [adj_flat[pl.ds(pl.multiple_of((c * half + at - 1 + xx) * adj_n, adj_n), adj_n), :]
                 for xx in range(2)], 1).astype(BF16)
            part = [lax.dot_general(basis, jnp.concatenate(halves[h], 0), (((1,), (1,)), ((), ())),
                                    preferred_element_type=F32) for h in range(2)]
            made = part if made is None else [made[h] + part[h] for h in range(2)]
        return made

    def sib_copy(n):
        return pltpu.make_async_remote_copy(
            acc.at[n, 0], sib_in.at[n], sib_send.at[n], sib_recv.at[n],
            device_id=(tx, ty, sib), device_id_type=MESH)

    def part_copy(off):
        to = lax.rem(me + off, group_n)
        to_x, to_y = to // ty_n, lax.rem(to, ty_n)
        return pltpu.make_async_remote_copy(
            stage.at[to_y, to_x], parts.at[me], part_send.at[off], part_recv.at[off],
            device_id=(to_x, to_y, pg), device_id_type=MESH)

    def chunk_of(n):
        return lax.rem(ty // per_chunk + 1 + n, chunks)

    def give(n):
        ch = chunk_of(n)
        sib_copy(n).wait_recv()
        block = (acc[n, 1] + sib_in[n]) * weight
        for i in range(per_chunk):
            to_y = ch * per_chunk + i
            for to_x in range(tx_n):
                piece = block[to_x * k_width:(to_x + 1) * k_width, i * width:(i + 1) * width]
                to = to_x * ty_n + to_y
                stage[to_y, to_x] = piece.astype(BF16)

                @pl.when(to != me)
                def _():
                    part_copy(lax.rem(to - me + group_n, group_n)).start()

                @pl.when(to == me)
                def _():
                    mine[...] = piece

    def arrive(t):
        for k in range(steps):
            @pl.when(t == k)
            def _():
                for off in range(1, pg_n):
                    mode_in(off, k).wait_recv()

        @pl.when(jnp.logical_and(t == steps - 1, gets_x))
        def _():
            for p in range(pg_n):
                x_in(p).wait_recv()

        grads(t)

    def unit(index, carry):
        later = jnp.maximum(index - chunks, 0)
        opening = index < chunks
        t = jnp.where(opening, 0, 1 + lax.rem(later, steps - 1))
        n = jnp.where(opening, index, later // (steps - 1))

        @pl.when(jnp.logical_or(index == 0, jnp.logical_and(index >= chunks, index < chunks + steps - 1)))
        def _():
            arrive(t)

        made = tensor(t, chunk_of(n))
        for h in range(2):
            acc[n, h] = jnp.where(t == 0, 0.0, acc[n, h]) + made[h]

        @pl.when(t == steps - 1)
        def _():
            sib_copy(n).start()

        @pl.when(jnp.logical_and(t == 1, n > 0))
        def _():
            give(n - 1)
        return carry

    lax.fori_loop(0, units, unit, 0)
    give(chunks - 1)

    for t in range(steps):
        for off in range(1, pg_n):
            mode_out(off, t).wait_send()
    for side, sends, _ in y_sides:
        @pl.when(sends)
        def _():
            for d in range(pg_n):
                y_out(side, d).wait_send()
    for side, sends in x_sides:
        @pl.when(sends)
        def _():
            for h in range(pg_n // 2):
                x_out(side, h).wait_send()
    for n in range(chunks):
        sib_copy(n).wait_send()
    for off in range(1, group_n):
        part_copy(off).wait()
    result = mine[...]
    for off in range(1, group_n):
        result = result + parts[lax.rem(me + off, group_n)].astype(F32)
    out_ref[...] = result


def shards(direct_modes, adjoint_modes, block_order):
    tx_n, ty_n, pg_n = lax.axis_size("tx"), lax.axis_size("ty"), lax.axis_size("pg")
    own_n, _, nx, lanes = direct_modes.shape
    adj_n = adjoint_modes.shape[0]
    mode_n = own_n * pg_n
    weight = 1.0 / math.sqrt(3.0 * nx * tx_n * lanes * ty_n)
    j_width, k_width = mode_n // ty_n, adj_n // tx_n
    blk = mode_n // NBLK
    half, width = nx // 2, j_width * own_n
    chunks = pg_n
    vmem = pl.BlockSpec(memory_space=pltpu.VMEM)
    dma = pltpu.SemaphoreType.DMA
    summed = pl.pallas_call(
        functools.partial(kernel, tx_n, ty_n, pg_n, weight),
        out_shape=jax.ShapeDtypeStruct((k_width, width), F32),
        in_specs=[pl.BlockSpec(memory_space=pltpu.SMEM)] + [pl.BlockSpec(memory_space=pl.ANY)] * 2,
        out_specs=vmem,
        scratch_shapes=[
            pltpu.VMEM((own_n, 3, nx, lanes), BF16),
            dma,
            pltpu.VMEM((nx * 3 * own_n, lanes), F32),
            pltpu.VMEM((nx, 3, own_n, lanes), BF16),
            pltpu.VMEM((adj_n, 3, nx, lanes), BF16),
            pltpu.VMEM((3 * half * adj_n, lanes), F32),
            dma,
            pltpu.VMEM((half + 2, pg_n, 3, own_n, lanes), BF16),
            pltpu.VMEM((2, 2, own_n, lanes), BF16),
            pltpu.VMEM((2, pg_n, own_n, lanes), BF16),
            pltpu.VMEM((half, 3, NBLK, blk, lanes), F32),
            pltpu.VMEM((half, 9, NBLK, blk, lanes), F32),
            pltpu.VMEM((half, 3, 2, own_n, lanes), WORK),
            pltpu.VMEM((half, 9, 2, own_n, lanes), WORK),
            pltpu.VMEM((chunks, 2, adj_n, own_n * own_n), F32),
            pltpu.VMEM((chunks, adj_n, own_n * own_n), F32),
            pltpu.VMEM((ty_n, tx_n, k_width, width), BF16),
            pltpu.VMEM((tx_n * ty_n, k_width, width), BF16),
            pltpu.VMEM((k_width, width), F32),
            dma((pg_n, half // 2)), dma((pg_n, half // 2)),
            dma((2, pg_n // 2)), dma((pg_n,)),
            dma((2, pg_n)), dma((2, pg_n)),
            dma((chunks,)), dma((chunks,)),
            dma((tx_n * ty_n,)), dma((tx_n * ty_n,)),
        ],
        compiler_params=pltpu.CompilerParams(
            collective_id=0, has_side_effects=True, vmem_limit_bytes=60 * 2**20),
    )(block_order, direct_modes, adjoint_modes)
    return jnp.transpose(summed.reshape(k_width, j_width, own_n), (2, 1, 0))


def solution(mesh):
    placed = (P("pg", None, "tx", "ty"), P(None, None, "tx", "ty"), P())
    return jax.shard_map(
        shards, mesh=mesh, in_specs=placed, out_specs=P("pg", "ty", "tx"), check_vma=False
    )
```

```python
import functools
import math

import jax
import jax.numpy as jnp
from jax import lax
from jax.experimental import pallas as pl
from jax.experimental.pallas import tpu as pltpu
from jax.sharding import PartitionSpec as P

NBLK = 8
CZ = 4
MESH = pl.DeviceIdType.MESH
F32 = jnp.float32
BF16 = jnp.bfloat16
WORK = BF16


def kernel(
    tx_n, ty_n, pg_n, weight,
    order_ref, own_any, adj_any, out_ref,
    own_in, own_sem, own_flat, own_ref, adj_raw, adj_flat, adj_sem, wide, face, edge, col_u, col_g, row_u, row_g,
    acc, sib_in, stage, parts, mine,
    mode_send, mode_recv, x_send, x_recv, y_send, y_recv, sib_send, sib_recv, part_send, part_recv, row_sem, col_sem,
):
    tx, ty, pg = lax.axis_index("tx"), lax.axis_index("ty"), lax.axis_index("pg")
    nx, _, own_n, lanes = own_ref.shape
    adj_n = adj_raw.shape[0]
    half = nx // 2
    steps = half // 2
    blk = pg_n * own_n // NBLK
    per_pair = 2 * NBLK // pg_n
    per_own = per_pair // 2
    co, hi = lax.rem(pg, 2), pg // 2
    sib = pg + 1 - 2 * co
    group_n = tx_n * ty_n
    me = tx * ty_n + ty

    own_copy = pltpu.make_async_copy(own_any, own_in, own_sem)
    own_copy.start()
    adj_copy = pltpu.make_async_copy(adj_any, adj_raw, adj_sem)
    adj_copy.start()

    has_xl, has_xh = tx > 0, tx < tx_n - 1
    has_yl, has_yh = ty > 0, ty < ty_n - 1

    barrier = pltpu.get_barrier_semaphore()
    for off in range(1, pg_n):
        pl.semaphore_signal(barrier, inc=1, device_id=(tx, ty, lax.rem(pg + off, pg_n)), device_id_type=MESH)
    for has, dx, dy in ((has_xl, -1, 0), (has_xh, 1, 0), (has_yl, 0, -1), (has_yh, 0, 1)):
        @pl.when(has)
        def _():
            for d in range(pg_n):
                pl.semaphore_signal(barrier, inc=1, device_id=(tx + dx, ty + dy, d), device_id_type=MESH)

    own_copy.wait()
    for m in range(own_n):
        for c in range(3):
            own_flat[pl.ds(c * own_n + m, nx, stride=3 * own_n), :] = own_in[m, c].astype(F32)
    for x in range(nx):
        for c in range(3):
            own_ref[x, c] = own_flat[pl.ds((x * 3 + c) * own_n, own_n), :].astype(BF16)

    neighbours = (has_xl.astype(jnp.int32) + has_xh.astype(jnp.int32)
                  + has_yl.astype(jnp.int32) + has_yh.astype(jnp.int32))
    pl.semaphore_wait(barrier, (pg_n - 1) + neighbours * pg_n)

    above, below = ty_n - 1 - ty, ty
    right, left = tx_n - 1 - tx, tx

    def tell_row(side, when):
        @pl.when(jnp.logical_and(when, (below if side == 0 else above) > 0))
        def _():
            pl.semaphore_signal(
                row_sem.at[side], inc=1, device_id=(tx, ty - 1 if side == 0 else ty + 1, pg), device_id_type=MESH)

    def tell_col(side, when):
        @pl.when(jnp.logical_and(when, (left if side == 0 else right) > 0))
        def _():
            pl.semaphore_signal(
                col_sem.at[side], inc=1, device_id=(tx - 1 if side == 0 else tx + 1, ty, pg), device_id_type=MESH)

    tell_row(0, above > 0)
    tell_row(1, below > 0)

    def pass_row():
        for j in range(1, ty_n - 1):
            for side, ahead, behind in ((0, above, below), (1, below, above)):
                @pl.when(jnp.logical_and(j < ahead, behind > 0))
                def _():
                    pl.semaphore_wait(row_sem.at[side], 1)
                    tell_row(side, True)

    def row_known():
        for side, ahead, behind in ((0, above, below), (1, below, above)):
            @pl.when(jnp.logical_and(ahead > 1, behind == 0))
            def _():
                pl.semaphore_wait(row_sem.at[side], ahead - 1)
        tell_col(0, True)
        tell_col(1, True)

    def all_known():
        for j in range(tx_n - 1):
            for side, ahead in ((0, right), (1, left)):
                @pl.when(j < ahead)
                def _():
                    pl.semaphore_wait(col_sem.at[side], 1)
                    tell_col(side, True)

    def span(t):
        return (0 if t == 0 else 2 + 2 * t), min(4 + 2 * t, half + 1)

    def mode_copy(off, t, src_pg, dst_pg):
        first, last = span(t)
        q = lax.rem(dst_pg, 2)
        at = q * first + (1 - q) * (half + 2 - last)
        return pltpu.make_async_remote_copy(
            own_ref.at[pl.ds(at + q * half - 1, last - first)], wide.at[pl.ds(at, last - first), src_pg],
            mode_send.at[off, t], mode_recv.at[off, t], device_id=(tx, ty, dst_pg), device_id_type=MESH)

    def mode_out(off, t):
        return mode_copy(off, t, pg, lax.rem(pg + off, pg_n))

    def mode_in(off, t):
        return mode_copy(off, t, lax.rem(pg + pg_n - off, pg_n), pg)

    def x_out(side, h):
        src, at, to = (nx - 1, 0, tx + 1) if side == 0 else (0, half + 1, tx - 1)
        return pltpu.make_async_remote_copy(
            own_ref.at[src], wide.at[at, pg], x_send.at[side, h], x_recv.at[pg],
            device_id=(to, ty, 2 * h + side), device_id_type=MESH)

    def x_in(source):
        return pltpu.make_async_remote_copy(
            own_ref.at[0], wide.at[co * (half + 1), source], x_send.at[0, 0], x_recv.at[source],
            device_id=(tx, ty, pg), device_id_type=MESH)

    def y_out(side, d):
        return pltpu.make_async_remote_copy(
            face.at[side, d % 2], edge.at[side, pg], y_send.at[side, d], y_recv.at[side, pg],
            device_id=(tx, ty + 1 - 2 * side, d), device_id_type=MESH)

    def y_in(side, source):
        return pltpu.make_async_remote_copy(
            face.at[side, 0], edge.at[side, source], y_send.at[side, 0], y_recv.at[side, source],
            device_id=(tx, ty, pg), device_id_type=MESH)

    y_sides = ((0, has_yh, has_yl), (1, has_yl, has_yh))
    x_sides = ((0, has_xh), (1, has_xl))
    gets_x = jnp.logical_or(jnp.logical_and(co == 0, has_xl), jnp.logical_and(co == 1, has_xh))
    far_first = [off for off in range(1, pg_n)]

    for off in far_first:
        mode_out(off, 0).start()

    lane = lax.broadcasted_iota(jnp.int32, (own_n, lanes), 1)
    for side in range(2):
        for q in range(2):
            packed = jnp.zeros((own_n, lanes), F32)
            for c in range(3):
                for i in range(half):
                    tile = own_ref[q * half + i, c].astype(F32)
                    at = (c * half + i) * CZ
                    shift = (at + (CZ if side == 0 else 0)) % lanes
                    here = (lane >= at) & (lane < at + CZ)
                    packed = jnp.where(here, pltpu.roll(tile, shift, 1) if shift else tile, packed)
            face[side, q] = packed.astype(BF16)
    for side, sends, _ in y_sides:
        @pl.when(sends)
        def _():
            for d in range(pg_n):
                y_out(side, d).start()
    for t in range(1, steps):
        for off in far_first:
            mode_out(off, t).start()
    for side, sends in x_sides:
        @pl.when(sends)
        def _():
            for h in range(pg_n // 2):
                x_out(side, h).start()

    wide[pl.ds(1 - co, half + 1), pg] = own_ref[pl.ds(co * (half - 1), half + 1)]

    @pl.when(jnp.logical_not(gets_x))
    def _():
        wide[co * (half + 1)] = jnp.zeros((pg_n, 3, own_n, lanes), BF16)

    for side, _, gets in y_sides:
        @pl.when(jnp.logical_not(gets))
        def _():
            edge[side] = jnp.zeros((pg_n, own_n, lanes), BF16)

    adj_copy.wait()

    def turn_basis(i, carry):
        for more in range(4):
            k = i * 4 + more
            for c in range(3):
                both = adj_raw[k, c].astype(F32)
                adj_flat[pl.ds(c * half * adj_n + k, half, stride=adj_n), :] = jnp.where(
                    co == 0, both[:half], both[half:])
        return carry

    lax.fori_loop(0, adj_n // 4, turn_basis, 0)

    for side, _, gets in y_sides:
        @pl.when(gets)
        def _():
            for p in range(pg_n):
                y_in(side, p).wait_recv()

    place = lax.rem(lane, CZ)
    tiles = own_n // blk

    def first_of(t):
        return co * (1 + 2 * t) + (1 - co) * (half - 1 - 2 * t)

    def grads(t):
        at = first_of(t)
        for xx in range(2):
            i, to = at + xx, 2 * t + xx
            for p in range(pg_n):
                for c in range(3):
                    u = wide[i, p, c].astype(F32)
                    col_u[to, c, pl.ds(p * tiles, tiles)] = u.reshape(tiles, blk, lanes)
                    gx = wide[i + 1, p, c].astype(F32) - wide[i - 1, p, c].astype(F32)
                    place_at = (c * half + i - 1) * CZ
                    e_hi = pltpu.roll(edge[1, p].astype(F32), lanes - CZ - place_at, 1)
                    e_lo = pltpu.roll(edge[0, p].astype(F32), lax.rem(lanes - place_at, lanes), 1)
                    up = jnp.where(lane >= lanes - CZ, e_hi, pltpu.roll(u, lanes - CZ, 1))
                    down = jnp.where(lane < CZ, e_lo, pltpu.roll(u, CZ, 1))
                    gy = up - down
                    upper = jnp.where(place == CZ - 1, pltpu.roll(u, CZ - 1, 1), pltpu.roll(u, lanes - 1, 1))
                    lower = jnp.where(place == 0, pltpu.roll(u, lanes - CZ + 1, 1), pltpu.roll(u, 1, 1))
                    gz = upper - lower
                    for d, g in enumerate((gx, gy, gz)):
                        g = (g * 0.5).astype(BF16).astype(F32)
                        col_g[to, d * 3 + c, pl.ds(p * tiles, tiles)] = g.reshape(tiles, blk, lanes)
            for h in range(2):
                group = lax.rem(co + 1 + h, 2)
                slots = [order_ref[hi * per_pair + group * per_own + b] for b in range(per_own)]
                for d in range(3):
                    row_u[to, d, h] = jnp.concatenate([col_u[to, d, s] for s in slots], 0).astype(WORK)
                for k in range(9):
                    row_g[to, k, h] = jnp.concatenate([col_g[to, k, s] for s in slots], 0).astype(WORK)

    chunk_j = own_n
    chunks = pg_n * own_n // chunk_j
    per_chunk = ty_n // chunks
    _, _, k_width, width = stage.shape
    units = chunks * steps

    def tensor(t, ch, parts_of):
        at = first_of(t)
        made = None
        for c in range(3):
            halves = [[] for _ in parts_of]
            for jj in range(chunk_j):
                jb, jr = ch * (chunk_j // blk) + jj // blk, pl.ds(jj % blk, 1)
                cells = [[] for _ in parts_of]
                for xx in range(2):
                    x = 2 * t + xx
                    ju = [jnp.broadcast_to(col_u[x, d, jb, jr], (own_n, lanes)).astype(WORK) for d in range(3)]
                    jg = [jnp.broadcast_to(col_g[x, d * 3 + c, jb, jr], (own_n, lanes)).astype(WORK)
                          for d in range(3)]
                    for i, h in enumerate(parts_of):
                        v = [jg[d] * row_u[x, d, h] for d in range(3)]
                        v += [ju[d] * row_g[x, d * 3 + c, h] for d in range(3)]
                        total = ((v[0] + v[3]) + (v[1] + v[4])) + (v[2] + v[5])
                        cells[i].append(total.astype(BF16))
                for i in range(len(parts_of)):
                    halves[i].append(jnp.concatenate(cells[i], 1))
            basis = jnp.concatenate(
                [adj_flat[pl.ds(pl.multiple_of((c * half + at - 1 + xx) * adj_n, adj_n), adj_n), :]
                 for xx in range(2)], 1).astype(BF16)
            part = [lax.dot_general(basis, jnp.concatenate(rows, 0), (((1,), (1,)), ((), ())),
                                    preferred_element_type=F32) for rows in halves]
            made = part if made is None else [m + p for m, p in zip(made, part)]
        return made

    def sib_copy(n):
        return pltpu.make_async_remote_copy(
            acc.at[n, 0], sib_in.at[n], sib_send.at[n], sib_recv.at[n],
            device_id=(tx, ty, sib), device_id_type=MESH)

    def part_copy(off):
        to = lax.rem(me + off, group_n)
        to_x, to_y = to // ty_n, lax.rem(to, ty_n)
        return pltpu.make_async_remote_copy(
            stage.at[to_y, to_x], parts.at[me], part_send.at[off], part_recv.at[off],
            device_id=(to_x, to_y, pg), device_id_type=MESH)

    def chunk_of(n):
        return lax.rem(n + jnp.minimum(ty // per_chunk + 2, chunks), chunks)

    def give(n):
        ch = chunk_of(n)
        sib_copy(n).wait_recv()
        block = (acc[n, 1] + sib_in[n]) * weight
        for i in range(per_chunk):
            to_y = ch * per_chunk + i
            for to_x in range(tx_n):
                piece = block[to_x * k_width:(to_x + 1) * k_width, i * width:(i + 1) * width]
                to = to_x * ty_n + to_y
                stage[to_y, to_x] = piece.astype(BF16)

                @pl.when(to != me)
                def _():
                    part_copy(lax.rem(to - me + group_n, group_n)).start()

                @pl.when(to == me)
                def _():
                    mine[...] = piece

    def arrive(t):
        for k in range(steps):
            @pl.when(t == k)
            def _():
                for off in range(1, pg_n):
                    mode_in(off, k).wait_recv()

        @pl.when(jnp.logical_and(t == steps - 1, gets_x))
        def _():
            for p in range(pg_n):
                x_in(p).wait_recv()

        grads(t)

    whole = chunks - 1
    rest = steps - 1

    def unit(index, carry):
        later = jnp.maximum(index - chunks, 0)
        opening = index < chunks
        t = jnp.where(opening, 0, 1 + lax.rem(later, rest))
        n = jnp.where(opening, index, later // rest)

        @pl.when(index == chunks)
        def _():
            row_known()

        @pl.when(jnp.logical_or(index == 0, jnp.logical_and(index >= chunks, index < chunks + rest)))
        def _():
            arrive(t)

        @pl.when(index == 0)
        def _():
            pass_row()

        made = tensor(t, chunk_of(n), (0, 1))
        for h in range(2):
            acc[n, h] = jnp.where(t == 0, 0.0, acc[n, h]) + made[h]

        @pl.when(t == steps - 1)
        def _():
            sib_copy(n).start()

        @pl.when(jnp.logical_and(t == 1, n == 1))
        def _():
            all_known()

        @pl.when(jnp.logical_and(t == 1, n > 0))
        def _():
            give(n - 1)
        return carry

    lax.fori_loop(0, chunks + whole * rest, unit, 0)

    def half_unit(index, carry):
        per_half = (chunks - whole) * rest
        h, inner = index // per_half, lax.rem(index, per_half)
        n, t = whole + inner // rest, 1 + lax.rem(inner, rest)
        made = tensor(t, chunk_of(n), (h,))
        acc[n, h] += made[0]

        @pl.when(index == 1)
        def _():
            give(whole - 1)

        @pl.when(jnp.logical_and(t == steps - 1, h == 0))
        def _():
            sib_copy(n).start()

        @pl.when(jnp.logical_and(t == steps - 1, h == 1))
        def _():
            give(n)
        return carry

    lax.fori_loop(0, 2 * (chunks - whole) * rest, half_unit, 0)

    for t in range(steps):
        for off in range(1, pg_n):
            mode_out(off, t).wait_send()
    for side, sends, _ in y_sides:
        @pl.when(sends)
        def _():
            for d in range(pg_n):
                y_out(side, d).wait_send()
    for side, sends in x_sides:
        @pl.when(sends)
        def _():
            for h in range(pg_n // 2):
                x_out(side, h).wait_send()
    for n in range(chunks):
        sib_copy(n).wait_send()
    for off in range(1, group_n):
        part_copy(off).wait()
    result = mine[...]
    for off in range(1, group_n):
        result = result + parts[lax.rem(me + off, group_n)].astype(F32)
    out_ref[...] = result


def shards(direct_modes, adjoint_modes, block_order):
    tx_n, ty_n, pg_n = lax.axis_size("tx"), lax.axis_size("ty"), lax.axis_size("pg")
    own_n, _, nx, lanes = direct_modes.shape
    adj_n = adjoint_modes.shape[0]
    mode_n = own_n * pg_n
    weight = 1.0 / math.sqrt(3.0 * nx * tx_n * lanes * ty_n)
    j_width, k_width = mode_n // ty_n, adj_n // tx_n
    blk = mode_n // NBLK
    half, width = nx // 2, j_width * own_n
    chunks = pg_n
    vmem = pl.BlockSpec(memory_space=pltpu.VMEM)
    dma = pltpu.SemaphoreType.DMA
    summed = pl.pallas_call(
        functools.partial(kernel, tx_n, ty_n, pg_n, weight),
        out_shape=jax.ShapeDtypeStruct((k_width, width), F32),
        in_specs=[pl.BlockSpec(memory_space=pltpu.SMEM)] + [pl.BlockSpec(memory_space=pl.ANY)] * 2,
        out_specs=vmem,
        scratch_shapes=[
            pltpu.VMEM((own_n, 3, nx, lanes), BF16),
            dma,
            pltpu.VMEM((nx * 3 * own_n, lanes), F32),
            pltpu.VMEM((nx, 3, own_n, lanes), BF16),
            pltpu.VMEM((adj_n, 3, nx, lanes), BF16),
            pltpu.VMEM((3 * half * adj_n, lanes), F32),
            dma,
            pltpu.VMEM((half + 2, pg_n, 3, own_n, lanes), BF16),
            pltpu.VMEM((2, 2, own_n, lanes), BF16),
            pltpu.VMEM((2, pg_n, own_n, lanes), BF16),
            pltpu.VMEM((half, 3, NBLK, blk, lanes), F32),
            pltpu.VMEM((half, 9, NBLK, blk, lanes), F32),
            pltpu.VMEM((half, 3, 2, own_n, lanes), WORK),
            pltpu.VMEM((half, 9, 2, own_n, lanes), WORK),
            pltpu.VMEM((chunks, 2, adj_n, own_n * own_n), F32),
            pltpu.VMEM((chunks, adj_n, own_n * own_n), F32),
            pltpu.VMEM((ty_n, tx_n, k_width, width), BF16),
            pltpu.VMEM((tx_n * ty_n, k_width, width), BF16),
            pltpu.VMEM((k_width, width), F32),
            dma((pg_n, half // 2)), dma((pg_n, half // 2)),
            dma((2, pg_n // 2)), dma((pg_n,)),
            dma((2, pg_n)), dma((2, pg_n)),
            dma((chunks,)), dma((chunks,)),
            dma((tx_n * ty_n,)), dma((tx_n * ty_n,)),
            pltpu.SemaphoreType.REGULAR((2,)), pltpu.SemaphoreType.REGULAR((2,)),
        ],
        compiler_params=pltpu.CompilerParams(
            collective_id=0, has_side_effects=True, vmem_limit_bytes=60 * 2**20),
    )(block_order, direct_modes, adjoint_modes)
    return jnp.transpose(summed.reshape(k_width, j_width, own_n), (2, 1, 0))


def solution(mesh):
    placed = (P("pg", None, "tx", "ty"), P(None, None, "tx", "ty"), P())
    return jax.shard_map(
        shards, mesh=mesh, in_specs=placed, out_specs=P("pg", "ty", "tx"), check_vma=False
    )
```

```python
import functools
import math

import jax
import jax.numpy as jnp
from jax import lax
from jax.experimental import pallas as pl
from jax.experimental.pallas import tpu as pltpu
from jax.sharding import PartitionSpec as P

NBLK = 8
CZ = 4
MESH = pl.DeviceIdType.MESH
F32 = jnp.float32
BF16 = jnp.bfloat16
WORK = BF16


def kernel(
    tx_n, ty_n, pg_n, weight,
    order_ref, own_any, adj_any, out_ref,
    own_in, own_sem, own_flat, own_ref, adj_raw, adj_flat, adj_sem, wide, face, edge, col_u, col_g, row_u, row_g,
    acc, sib_in, stage, parts, mine,
    mode_send, mode_recv, x_send, x_recv, y_send, y_recv, sib_send, sib_recv, part_send, part_recv, row_sem, col_sem,
):
    tx, ty, pg = lax.axis_index("tx"), lax.axis_index("ty"), lax.axis_index("pg")
    nx, _, own_n, lanes = own_ref.shape
    adj_n = adj_raw.shape[0]
    half = nx // 2
    steps = half // 2
    blk = pg_n * own_n // NBLK
    per_pair = 2 * NBLK // pg_n
    per_own = per_pair // 2
    co, hi = lax.rem(pg, 2), pg // 2
    sib = pg + 1 - 2 * co
    group_n = tx_n * ty_n
    me = tx * ty_n + ty

    own_copy = pltpu.make_async_copy(own_any, own_in, own_sem)
    own_copy.start()
    adj_copy = pltpu.make_async_copy(adj_any, adj_raw, adj_sem)
    adj_copy.start()

    has_xl, has_xh = tx > 0, tx < tx_n - 1
    has_yl, has_yh = ty > 0, ty < ty_n - 1

    barrier = pltpu.get_barrier_semaphore()
    for off in range(1, pg_n):
        pl.semaphore_signal(barrier, inc=1, device_id=(tx, ty, lax.rem(pg + off, pg_n)), device_id_type=MESH)
    for has, dx, dy in ((has_xl, -1, 0), (has_xh, 1, 0), (has_yl, 0, -1), (has_yh, 0, 1)):
        @pl.when(has)
        def _():
            for d in range(pg_n):
                pl.semaphore_signal(barrier, inc=1, device_id=(tx + dx, ty + dy, d), device_id_type=MESH)

    own_copy.wait()
    for m in range(own_n):
        for c in range(3):
            own_flat[pl.ds(c * own_n + m, nx, stride=3 * own_n), :] = own_in[m, c].astype(F32)
    for x in range(nx):
        for c in range(3):
            own_ref[x, c] = own_flat[pl.ds((x * 3 + c) * own_n, own_n), :].astype(BF16)

    neighbours = (has_xl.astype(jnp.int32) + has_xh.astype(jnp.int32)
                  + has_yl.astype(jnp.int32) + has_yh.astype(jnp.int32))
    pl.semaphore_wait(barrier, (pg_n - 1) + neighbours * pg_n)

    above, below = ty_n - 1 - ty, ty
    right, left = tx_n - 1 - tx, tx

    def tell_row(side, when):
        @pl.when(jnp.logical_and(when, (below if side == 0 else above) > 0))
        def _():
            pl.semaphore_signal(
                row_sem.at[side], inc=1, device_id=(tx, ty - 1 if side == 0 else ty + 1, pg), device_id_type=MESH)

    def tell_col(side, when):
        @pl.when(jnp.logical_and(when, (left if side == 0 else right) > 0))
        def _():
            pl.semaphore_signal(
                col_sem.at[side], inc=1, device_id=(tx - 1 if side == 0 else tx + 1, ty, pg), device_id_type=MESH)

    tell_row(0, above > 0)
    tell_row(1, below > 0)

    def pass_row():
        for j in range(1, ty_n - 1):
            for side, ahead, behind in ((0, above, below), (1, below, above)):
                @pl.when(jnp.logical_and(j < ahead, behind > 0))
                def _():
                    pl.semaphore_wait(row_sem.at[side], 1)
                    tell_row(side, True)

    def row_known():
        for side, ahead, behind in ((0, above, below), (1, below, above)):
            @pl.when(jnp.logical_and(ahead > 1, behind == 0))
            def _():
                pl.semaphore_wait(row_sem.at[side], ahead - 1)
        tell_col(0, True)
        tell_col(1, True)

    def all_known():
        for j in range(tx_n - 1):
            for side, ahead in ((0, right), (1, left)):
                @pl.when(j < ahead)
                def _():
                    pl.semaphore_wait(col_sem.at[side], 1)
                    tell_col(side, True)

    def span(t):
        return (0 if t == 0 else 2 + 2 * t), min(4 + 2 * t, half + 1)

    def mode_copy(off, t, src_pg, dst_pg):
        first, last = span(t)
        q = lax.rem(dst_pg, 2)
        at = q * first + (1 - q) * (half + 2 - last)
        return pltpu.make_async_remote_copy(
            own_ref.at[pl.ds(at + q * half - 1, last - first)], wide.at[pl.ds(at, last - first), src_pg],
            mode_send.at[off, t], mode_recv.at[off, t], device_id=(tx, ty, dst_pg), device_id_type=MESH)

    def mode_out(off, t):
        return mode_copy(off, t, pg, lax.rem(pg + off, pg_n))

    def mode_in(off, t):
        return mode_copy(off, t, lax.rem(pg + pg_n - off, pg_n), pg)

    def x_out(side, h):
        src, at, to = (nx - 1, 0, tx + 1) if side == 0 else (0, half + 1, tx - 1)
        return pltpu.make_async_remote_copy(
            own_ref.at[src], wide.at[at, pg], x_send.at[side, h], x_recv.at[pg],
            device_id=(to, ty, 2 * h + side), device_id_type=MESH)

    def x_in(source):
        return pltpu.make_async_remote_copy(
            own_ref.at[0], wide.at[co * (half + 1), source], x_send.at[0, 0], x_recv.at[source],
            device_id=(tx, ty, pg), device_id_type=MESH)

    def y_out(side, d):
        return pltpu.make_async_remote_copy(
            face.at[side, d % 2], edge.at[side, pg], y_send.at[side, d], y_recv.at[side, pg],
            device_id=(tx, ty + 1 - 2 * side, d), device_id_type=MESH)

    def y_in(side, source):
        return pltpu.make_async_remote_copy(
            face.at[side, 0], edge.at[side, source], y_send.at[side, 0], y_recv.at[side, source],
            device_id=(tx, ty, pg), device_id_type=MESH)

    y_sides = ((0, has_yh, has_yl), (1, has_yl, has_yh))
    x_sides = ((0, has_xh), (1, has_xl))
    gets_x = jnp.logical_or(jnp.logical_and(co == 0, has_xl), jnp.logical_and(co == 1, has_xh))
    far_first = [off for off in range(1, pg_n)]

    for off in far_first:
        mode_out(off, 0).start()

    lane = lax.broadcasted_iota(jnp.int32, (own_n, lanes), 1)
    for side in range(2):
        for q in range(2):
            packed = jnp.zeros((own_n, lanes), F32)
            for c in range(3):
                for i in range(half):
                    tile = own_ref[q * half + i, c].astype(F32)
                    at = (c * half + i) * CZ
                    shift = (at + (CZ if side == 0 else 0)) % lanes
                    here = (lane >= at) & (lane < at + CZ)
                    packed = jnp.where(here, pltpu.roll(tile, shift, 1) if shift else tile, packed)
            face[side, q] = packed.astype(BF16)
    for side, sends, _ in y_sides:
        @pl.when(sends)
        def _():
            for d in range(pg_n):
                y_out(side, d).start()
    for t in range(1, steps):
        for off in far_first:
            mode_out(off, t).start()
    for side, sends in x_sides:
        @pl.when(sends)
        def _():
            for h in range(pg_n // 2):
                x_out(side, h).start()

    wide[pl.ds(1 - co, half + 1), pg] = own_ref[pl.ds(co * (half - 1), half + 1)]

    @pl.when(jnp.logical_not(gets_x))
    def _():
        wide[co * (half + 1)] = jnp.zeros((pg_n, 3, own_n, lanes), BF16)

    for side, _, gets in y_sides:
        @pl.when(jnp.logical_not(gets))
        def _():
            edge[side] = jnp.zeros((pg_n, own_n, lanes), BF16)

    adj_copy.wait()

    def turn_basis(i, carry):
        for more in range(4):
            k = i * 4 + more
            for c in range(3):
                both = adj_raw[k, c].astype(F32)
                adj_flat[pl.ds(c * half * adj_n + k, half, stride=adj_n), :] = jnp.where(
                    co == 0, both[:half], both[half:])
        return carry

    lax.fori_loop(0, adj_n // 4, turn_basis, 0)

    for side, _, gets in y_sides:
        @pl.when(gets)
        def _():
            for p in range(pg_n):
                y_in(side, p).wait_recv()

    place = lax.rem(lane, CZ)
    tiles = own_n // blk

    def first_of(t):
        return co * (1 + 2 * t) + (1 - co) * (half - 1 - 2 * t)

    def grads(t):
        at = first_of(t)
        for xx in range(2):
            i, to = at + xx, 2 * t + xx
            for p in range(pg_n):
                for c in range(3):
                    u = wide[i, p, c].astype(F32)
                    col_u[to, c, pl.ds(p * tiles, tiles)] = u.reshape(tiles, blk, lanes)
                    gx = wide[i + 1, p, c].astype(F32) - wide[i - 1, p, c].astype(F32)
                    place_at = (c * half + i - 1) * CZ
                    e_hi = pltpu.roll(edge[1, p].astype(F32), lanes - CZ - place_at, 1)
                    e_lo = pltpu.roll(edge[0, p].astype(F32), lax.rem(lanes - place_at, lanes), 1)
                    up = jnp.where(lane >= lanes - CZ, e_hi, pltpu.roll(u, lanes - CZ, 1))
                    down = jnp.where(lane < CZ, e_lo, pltpu.roll(u, CZ, 1))
                    gy = up - down
                    upper = jnp.where(place == CZ - 1, pltpu.roll(u, CZ - 1, 1), pltpu.roll(u, lanes - 1, 1))
                    lower = jnp.where(place == 0, pltpu.roll(u, lanes - CZ + 1, 1), pltpu.roll(u, 1, 1))
                    gz = upper - lower
                    for d, g in enumerate((gx, gy, gz)):
                        g = (g * 0.5).astype(BF16).astype(F32)
                        col_g[to, d * 3 + c, pl.ds(p * tiles, tiles)] = g.reshape(tiles, blk, lanes)
            for h in range(2):
                group = lax.rem(co + 1 + h, 2)
                slots = [order_ref[hi * per_pair + group * per_own + b] for b in range(per_own)]
                for d in range(3):
                    row_u[to, d, h] = jnp.concatenate([col_u[to, d, s] for s in slots], 0).astype(WORK)
                for k in range(9):
                    row_g[to, k, h] = jnp.concatenate([col_g[to, k, s] for s in slots], 0).astype(WORK)

    chunk_j = own_n
    chunks = pg_n * own_n // chunk_j
    per_chunk = ty_n // chunks
    _, _, k_width, width = stage.shape
    units = chunks * steps

    def tensor(planes, ch, parts_of):
        made = [None for _ in parts_of]
        for t in planes:
            for c in range(3):
                halves = [[] for _ in parts_of]
                for jj in range(chunk_j):
                    jb, jr = ch * (chunk_j // blk) + jj // blk, pl.ds(jj % blk, 1)
                    cells = [[] for _ in parts_of]
                    for xx in range(2):
                        x = 2 * t + xx
                        ju = [jnp.broadcast_to(col_u[x, d, jb, jr], (own_n, lanes)).astype(WORK) for d in range(3)]
                        jg = [jnp.broadcast_to(col_g[x, d * 3 + c, jb, jr], (own_n, lanes)).astype(WORK)
                              for d in range(3)]
                        for i, h in enumerate(parts_of):
                            v = [jg[d] * row_u[x, d, h] for d in range(3)]
                            v += [ju[d] * row_g[x, d * 3 + c, h] for d in range(3)]
                            total = ((v[0] + v[3]) + (v[1] + v[4])) + (v[2] + v[5])
                            cells[i].append(total.astype(BF16))
                    for i in range(len(parts_of)):
                        halves[i].append(jnp.concatenate(cells[i], 1))
                basis = jnp.concatenate(
                    [adj_flat[pl.ds(pl.multiple_of((c * half + first_of(t) - 1 + xx) * adj_n, adj_n), adj_n), :]
                     for xx in range(2)], 1).astype(BF16)
                for i, rows in enumerate(halves):
                    part = lax.dot_general(basis, jnp.concatenate(rows, 0), (((1,), (1,)), ((), ())),
                                           preferred_element_type=F32)
                    made[i] = part if made[i] is None else made[i] + part
        return made

    def sib_copy(n):
        return pltpu.make_async_remote_copy(
            acc.at[n, 0], sib_in.at[n], sib_send.at[n], sib_recv.at[n],
            device_id=(tx, ty, sib), device_id_type=MESH)

    def part_copy(off):
        to = lax.rem(me + off, group_n)
        to_x, to_y = to // ty_n, lax.rem(to, ty_n)
        return pltpu.make_async_remote_copy(
            stage.at[to_y, to_x], parts.at[me], part_send.at[off], part_recv.at[off],
            device_id=(to_x, to_y, pg), device_id_type=MESH)

    def chunk_of(n):
        return n

    def give(n):
        ch = chunk_of(n)
        sib_copy(n).wait_recv()
        block = (acc[n, 1] + sib_in[n]) * weight
        for i in range(per_chunk):
            to_y = ch * per_chunk + i
            for to_x in range(tx_n):
                piece = block[to_x * k_width:(to_x + 1) * k_width, i * width:(i + 1) * width]
                to = to_x * ty_n + to_y
                stage[to_y, to_x] = piece.astype(BF16)

                @pl.when(to != me)
                def _():
                    part_copy(lax.rem(to - me + group_n, group_n)).start()

                @pl.when(to == me)
                def _():
                    mine[...] = piece

    def arrive(t):
        for k in range(steps):
            @pl.when(t == k)
            def _():
                for off in range(1, pg_n):
                    mode_in(off, k).wait_recv()

        @pl.when(jnp.logical_and(t == steps - 1, gets_x))
        def _():
            for p in range(pg_n):
                x_in(p).wait_recv()

        grads(t)

    whole = chunks - 1
    later = list(range(1, steps))

    arrive(0)
    pass_row()

    def open_two(i, carry):
        made = [tensor([0], chunk_of(2 * i + k), (0, 1)) for k in range(2)]
        for k in range(2):
            for h in range(2):
                acc[2 * i + k, h] = made[k][h]
        return carry

    lax.fori_loop(0, chunks // 2, open_two, 0)
    row_known()

    def arrive_later(t, carry):
        arrive(t)
        return carry

    lax.fori_loop(1, steps, arrive_later, 0)

    def finish(n, carry):
        made = tensor(later, chunk_of(n), (0, 1))
        for h in range(2):
            acc[n, h] += made[h]
        sib_copy(n).start()

        @pl.when(n == 0)
        def _():
            all_known()

        @pl.when(n > 0)
        def _():
            give(n - 1)
        return carry

    lax.fori_loop(0, whole, finish, 0)

    def finish_half(h, carry):
        acc[whole, h] += tensor(later, chunk_of(whole), (h,))[0]

        @pl.when(h == 0)
        def _():
            sib_copy(whole).start()
            give(whole - 1)
        return carry

    lax.fori_loop(0, 2, finish_half, 0)
    give(whole)

    for t in range(steps):
        for off in range(1, pg_n):
            mode_out(off, t).wait_send()
    for side, sends, _ in y_sides:
        @pl.when(sends)
        def _():
            for d in range(pg_n):
                y_out(side, d).wait_send()
    for side, sends in x_sides:
        @pl.when(sends)
        def _():
            for h in range(pg_n // 2):
                x_out(side, h).wait_send()
    for n in range(chunks):
        sib_copy(n).wait_send()
    for off in range(1, group_n):
        part_copy(off).wait()
    result = mine[...]
    for off in range(1, group_n):
        result = result + parts[lax.rem(me + off, group_n)].astype(F32)
    out_ref[...] = result


def shards(direct_modes, adjoint_modes, block_order):
    tx_n, ty_n, pg_n = lax.axis_size("tx"), lax.axis_size("ty"), lax.axis_size("pg")
    own_n, _, nx, lanes = direct_modes.shape
    adj_n = adjoint_modes.shape[0]
    mode_n = own_n * pg_n
    weight = 1.0 / math.sqrt(3.0 * nx * tx_n * lanes * ty_n)
    j_width, k_width = mode_n // ty_n, adj_n // tx_n
    blk = mode_n // NBLK
    half, width = nx // 2, j_width * own_n
    chunks = pg_n
    vmem = pl.BlockSpec(memory_space=pltpu.VMEM)
    dma = pltpu.SemaphoreType.DMA
    summed = pl.pallas_call(
        functools.partial(kernel, tx_n, ty_n, pg_n, weight),
        out_shape=jax.ShapeDtypeStruct((k_width, width), F32),
        in_specs=[pl.BlockSpec(memory_space=pltpu.SMEM)] + [pl.BlockSpec(memory_space=pl.ANY)] * 2,
        out_specs=vmem,
        scratch_shapes=[
            pltpu.VMEM((own_n, 3, nx, lanes), BF16),
            dma,
            pltpu.VMEM((nx * 3 * own_n, lanes), F32),
            pltpu.VMEM((nx, 3, own_n, lanes), BF16),
            pltpu.VMEM((adj_n, 3, nx, lanes), BF16),
            pltpu.VMEM((3 * half * adj_n, lanes), F32),
            dma,
            pltpu.VMEM((half + 2, pg_n, 3, own_n, lanes), BF16),
            pltpu.VMEM((2, 2, own_n, lanes), BF16),
            pltpu.VMEM((2, pg_n, own_n, lanes), BF16),
            pltpu.VMEM((half, 3, NBLK, blk, lanes), F32),
            pltpu.VMEM((half, 9, NBLK, blk, lanes), F32),
            pltpu.VMEM((half, 3, 2, own_n, lanes), WORK),
            pltpu.VMEM((half, 9, 2, own_n, lanes), WORK),
            pltpu.VMEM((chunks, 2, adj_n, own_n * own_n), F32),
            pltpu.VMEM((chunks, adj_n, own_n * own_n), F32),
            pltpu.VMEM((ty_n, tx_n, k_width, width), BF16),
            pltpu.VMEM((tx_n * ty_n, k_width, width), BF16),
            pltpu.VMEM((k_width, width), F32),
            dma((pg_n, half // 2)), dma((pg_n, half // 2)),
            dma((2, pg_n // 2)), dma((pg_n,)),
            dma((2, pg_n)), dma((2, pg_n)),
            dma((chunks,)), dma((chunks,)),
            dma((tx_n * ty_n,)), dma((tx_n * ty_n,)),
            pltpu.SemaphoreType.REGULAR((2,)), pltpu.SemaphoreType.REGULAR((2,)),
        ],
        compiler_params=pltpu.CompilerParams(
            collective_id=0, has_side_effects=True, vmem_limit_bytes=60 * 2**20),
    )(block_order, direct_modes, adjoint_modes)
    return jnp.transpose(summed.reshape(k_width, j_width, own_n), (2, 1, 0))


def solution(mesh):
    placed = (P("pg", None, "tx", "ty"), P(None, None, "tx", "ty"), P())
    return jax.shard_map(
        shards, mesh=mesh, in_specs=placed, out_specs=P("pg", "ty", "tx"), check_vma=False
    )
```

```python
import functools
import math

import jax
import jax.numpy as jnp
from jax import lax
from jax.experimental import pallas as pl
from jax.experimental.pallas import tpu as pltpu
from jax.sharding import PartitionSpec as P

NBLK = 8
CZ = 4
MESH = pl.DeviceIdType.MESH
F32 = jnp.float32
BF16 = jnp.bfloat16
WORK = BF16


def kernel(
    tx_n, ty_n, pg_n, weight,
    order_ref, own_any, adj_any, out_ref,
    own_in, own_sem, own_flat, own_ref, adj_raw, adj_flat, adj_sem, wide, face, edge, col_u, col_g, row_u, row_g,
    acc, sib_in, stage, parts, mine,
    mode_send, mode_recv, x_send, x_recv, y_send, y_recv, sib_send, sib_recv, part_send, part_recv, row_sem, col_sem,
):
    tx, ty, pg = lax.axis_index("tx"), lax.axis_index("ty"), lax.axis_index("pg")
    nx, _, own_n, lanes = own_ref.shape
    adj_n = adj_raw.shape[0]
    half = nx // 2
    steps = half // 2
    blk = pg_n * own_n // NBLK
    per_pair = 2 * NBLK // pg_n
    per_own = per_pair // 2
    co, hi = lax.rem(pg, 2), pg // 2
    sib = pg + 1 - 2 * co
    group_n = tx_n * ty_n
    me = tx * ty_n + ty

    own_copy = pltpu.make_async_copy(own_any, own_in, own_sem)
    own_copy.start()
    adj_copy = pltpu.make_async_copy(adj_any, adj_raw, adj_sem)
    adj_copy.start()

    has_xl, has_xh = tx > 0, tx < tx_n - 1
    has_yl, has_yh = ty > 0, ty < ty_n - 1

    barrier = pltpu.get_barrier_semaphore()
    for off in range(1, pg_n):
        pl.semaphore_signal(barrier, inc=1, device_id=(tx, ty, lax.rem(pg + off, pg_n)), device_id_type=MESH)
    for has, dx, dy in ((has_xl, -1, 0), (has_xh, 1, 0), (has_yl, 0, -1), (has_yh, 0, 1)):
        @pl.when(has)
        def _():
            for d in range(pg_n):
                pl.semaphore_signal(barrier, inc=1, device_id=(tx + dx, ty + dy, d), device_id_type=MESH)

    own_copy.wait()
    for m in range(own_n):
        for c in range(3):
            own_flat[pl.ds(c * own_n + m, nx, stride=3 * own_n), :] = own_in[m, c].astype(F32)
    for x in range(nx):
        for c in range(3):
            own_ref[x, c] = own_flat[pl.ds((x * 3 + c) * own_n, own_n), :].astype(BF16)

    neighbours = (has_xl.astype(jnp.int32) + has_xh.astype(jnp.int32)
                  + has_yl.astype(jnp.int32) + has_yh.astype(jnp.int32))
    pl.semaphore_wait(barrier, (pg_n - 1) + neighbours * pg_n)

    above, below = ty_n - 1 - ty, ty
    right, left = tx_n - 1 - tx, tx

    def tell_row(side, when):
        @pl.when(jnp.logical_and(when, (below if side == 0 else above) > 0))
        def _():
            pl.semaphore_signal(
                row_sem.at[side], inc=1, device_id=(tx, ty - 1 if side == 0 else ty + 1, pg), device_id_type=MESH)

    def tell_col(side, when):
        @pl.when(jnp.logical_and(when, (left if side == 0 else right) > 0))
        def _():
            pl.semaphore_signal(
                col_sem.at[side], inc=1, device_id=(tx - 1 if side == 0 else tx + 1, ty, pg), device_id_type=MESH)

    tell_row(0, above > 0)
    tell_row(1, below > 0)

    def pass_row():
        for j in range(1, ty_n - 1):
            for side, ahead, behind in ((0, above, below), (1, below, above)):
                @pl.when(jnp.logical_and(j < ahead, behind > 0))
                def _():
                    pl.semaphore_wait(row_sem.at[side], 1)
                    tell_row(side, True)

    def row_known():
        for side, ahead, behind in ((0, above, below), (1, below, above)):
            @pl.when(jnp.logical_and(ahead > 1, behind == 0))
            def _():
                pl.semaphore_wait(row_sem.at[side], ahead - 1)
        tell_col(0, True)
        tell_col(1, True)

    def all_known():
        for j in range(tx_n - 1):
            for side, ahead in ((0, right), (1, left)):
                @pl.when(j < ahead)
                def _():
                    pl.semaphore_wait(col_sem.at[side], 1)
                    tell_col(side, True)

    def span(t):
        return (0 if t == 0 else 2 + 2 * t), min(4 + 2 * t, half + 1)

    def mode_copy(off, t, src_pg, dst_pg):
        first, last = span(t)
        q = lax.rem(dst_pg, 2)
        at = q * first + (1 - q) * (half + 2 - last)
        return pltpu.make_async_remote_copy(
            own_ref.at[pl.ds(at + q * half - 1, last - first)], wide.at[pl.ds(at, last - first), src_pg],
            mode_send.at[off, t], mode_recv.at[off, t], device_id=(tx, ty, dst_pg), device_id_type=MESH)

    def mode_out(off, t):
        return mode_copy(off, t, pg, lax.rem(pg + off, pg_n))

    def mode_in(off, t):
        return mode_copy(off, t, lax.rem(pg + pg_n - off, pg_n), pg)

    def x_out(side, h):
        src, at, to = (nx - 1, 0, tx + 1) if side == 0 else (0, half + 1, tx - 1)
        return pltpu.make_async_remote_copy(
            own_ref.at[src], wide.at[at, pg], x_send.at[side, h], x_recv.at[pg],
            device_id=(to, ty, 2 * h + side), device_id_type=MESH)

    def x_in(source):
        return pltpu.make_async_remote_copy(
            own_ref.at[0], wide.at[co * (half + 1), source], x_send.at[0, 0], x_recv.at[source],
            device_id=(tx, ty, pg), device_id_type=MESH)

    def y_out(side, d):
        return pltpu.make_async_remote_copy(
            face.at[side, d % 2], edge.at[side, pg], y_send.at[side, d], y_recv.at[side, pg],
            device_id=(tx, ty + 1 - 2 * side, d), device_id_type=MESH)

    def y_in(side, source):
        return pltpu.make_async_remote_copy(
            face.at[side, 0], edge.at[side, source], y_send.at[side, 0], y_recv.at[side, source],
            device_id=(tx, ty, pg), device_id_type=MESH)

    y_sides = ((0, has_yh, has_yl), (1, has_yl, has_yh))
    x_sides = ((0, has_xh), (1, has_xl))
    gets_x = jnp.logical_or(jnp.logical_and(co == 0, has_xl), jnp.logical_and(co == 1, has_xh))
    far_first = [off for off in range(1, pg_n)]

    for off in far_first:
        mode_out(off, 0).start()

    lane = lax.broadcasted_iota(jnp.int32, (own_n, lanes), 1)
    for side in range(2):
        for q in range(2):
            packed = jnp.zeros((own_n, lanes), F32)
            for c in range(3):
                for i in range(half):
                    tile = own_ref[q * half + i, c].astype(F32)
                    at = (c * half + i) * CZ
                    shift = (at + (CZ if side == 0 else 0)) % lanes
                    here = (lane >= at) & (lane < at + CZ)
                    packed = jnp.where(here, pltpu.roll(tile, shift, 1) if shift else tile, packed)
            face[side, q] = packed.astype(BF16)
    for side, sends, _ in y_sides:
        @pl.when(sends)
        def _():
            for d in range(pg_n):
                y_out(side, d).start()
    for t in range(1, steps):
        for off in far_first:
            mode_out(off, t).start()
    for side, sends in x_sides:
        @pl.when(sends)
        def _():
            for h in range(pg_n // 2):
                x_out(side, h).start()

    wide[pl.ds(1 - co, half + 1), pg] = own_ref[pl.ds(co * (half - 1), half + 1)]

    @pl.when(jnp.logical_not(gets_x))
    def _():
        wide[co * (half + 1)] = jnp.zeros((pg_n, 3, own_n, lanes), BF16)

    for side, _, gets in y_sides:
        @pl.when(jnp.logical_not(gets))
        def _():
            edge[side] = jnp.zeros((pg_n, own_n, lanes), BF16)

    adj_copy.wait()

    def turn_basis(i, carry):
        for more in range(4):
            k = i * 4 + more
            for c in range(3):
                both = adj_raw[k, c].astype(F32)
                adj_flat[pl.ds(c * half * adj_n + k, half, stride=adj_n), :] = jnp.where(
                    co == 0, both[:half], both[half:])
        return carry

    lax.fori_loop(0, adj_n // 4, turn_basis, 0)

    for side, _, gets in y_sides:
        @pl.when(gets)
        def _():
            for p in range(pg_n):
                y_in(side, p).wait_recv()

    place = lax.rem(lane, CZ)
    tiles = own_n // blk

    def first_of(t):
        return co * (1 + 2 * t) + (1 - co) * (half - 1 - 2 * t)

    def grads(t):
        at = first_of(t)
        for xx in range(2):
            i, to = at + xx, 2 * t + xx
            for p in range(pg_n):
                for c in range(3):
                    u = wide[i, p, c].astype(F32)
                    col_u[to, c, pl.ds(p * tiles, tiles)] = u.reshape(tiles, blk, lanes)
                    gx = wide[i + 1, p, c].astype(F32) - wide[i - 1, p, c].astype(F32)
                    place_at = (c * half + i - 1) * CZ
                    e_hi = pltpu.roll(edge[1, p].astype(F32), lanes - CZ - place_at, 1)
                    e_lo = pltpu.roll(edge[0, p].astype(F32), lax.rem(lanes - place_at, lanes), 1)
                    up = jnp.where(lane >= lanes - CZ, e_hi, pltpu.roll(u, lanes - CZ, 1))
                    down = jnp.where(lane < CZ, e_lo, pltpu.roll(u, CZ, 1))
                    gy = up - down
                    upper = jnp.where(place == CZ - 1, pltpu.roll(u, CZ - 1, 1), pltpu.roll(u, lanes - 1, 1))
                    lower = jnp.where(place == 0, pltpu.roll(u, lanes - CZ + 1, 1), pltpu.roll(u, 1, 1))
                    gz = upper - lower
                    for d, g in enumerate((gx, gy, gz)):
                        g = (g * 0.5).astype(BF16).astype(F32)
                        col_g[to, d * 3 + c, pl.ds(p * tiles, tiles)] = g.reshape(tiles, blk, lanes)
            for h in range(2):
                group = lax.rem(co + 1 + h, 2)
                slots = [order_ref[hi * per_pair + group * per_own + b] for b in range(per_own)]
                for d in range(3):
                    row_u[to, d, h] = jnp.concatenate([col_u[to, d, s] for s in slots], 0).astype(WORK)
                for k in range(9):
                    row_g[to, k, h] = jnp.concatenate([col_g[to, k, s] for s in slots], 0).astype(WORK)

    chunk_j = own_n
    chunks = pg_n * own_n // chunk_j
    per_chunk = ty_n // chunks
    _, _, k_width, width = stage.shape
    units = chunks * steps

    def tensor(planes, ch, parts_of):
        made = [None for _ in parts_of]
        for t in planes:
            for c in range(3):
                halves = [[] for _ in parts_of]
                for jj in range(chunk_j):
                    jb, jr = ch * (chunk_j // blk) + jj // blk, pl.ds(jj % blk, 1)
                    cells = [[] for _ in parts_of]
                    for xx in range(2):
                        x = 2 * t + xx
                        ju = [jnp.broadcast_to(col_u[x, d, jb, jr], (own_n, lanes)).astype(WORK) for d in range(3)]
                        jg = [jnp.broadcast_to(col_g[x, d * 3 + c, jb, jr], (own_n, lanes)).astype(WORK)
                              for d in range(3)]
                        for i, h in enumerate(parts_of):
                            v = [jg[d] * row_u[x, d, h] for d in range(3)]
                            v += [ju[d] * row_g[x, d * 3 + c, h] for d in range(3)]
                            total = ((v[0] + v[3]) + (v[1] + v[4])) + (v[2] + v[5])
                            cells[i].append(total.astype(BF16))
                    for i in range(len(parts_of)):
                        halves[i].append(jnp.concatenate(cells[i], 1))
                basis = jnp.concatenate(
                    [adj_flat[pl.ds(pl.multiple_of((c * half + first_of(t) - 1 + xx) * adj_n, adj_n), adj_n), :]
                     for xx in range(2)], 1).astype(BF16)
                for i, rows in enumerate(halves):
                    part = lax.dot_general(basis, jnp.concatenate(rows, 0), (((1,), (1,)), ((), ())),
                                           preferred_element_type=F32)
                    made[i] = part if made[i] is None else made[i] + part
        return made

    def sib_copy(n):
        return pltpu.make_async_remote_copy(
            acc.at[n, 0], sib_in.at[n], sib_send.at[n], sib_recv.at[n],
            device_id=(tx, ty, sib), device_id_type=MESH)

    def part_copy(off):
        to = lax.rem(me + off, group_n)
        to_x, to_y = to // ty_n, lax.rem(to, ty_n)
        return pltpu.make_async_remote_copy(
            stage.at[to_y, to_x], parts.at[me], part_send.at[off], part_recv.at[off],
            device_id=(to_x, to_y, pg), device_id_type=MESH)

    def chunk_of(n):
        return n

    def give(n):
        ch = chunk_of(n)
        sib_copy(n).wait_recv()
        block = (acc[n, 1] + sib_in[n]) * weight
        for i in range(per_chunk):
            to_y = ch * per_chunk + i
            for to_x in range(tx_n):
                piece = block[to_x * k_width:(to_x + 1) * k_width, i * width:(i + 1) * width]
                to = to_x * ty_n + to_y
                stage[to_y, to_x] = piece.astype(BF16)

                @pl.when(to != me)
                def _():
                    part_copy(lax.rem(to - me + group_n, group_n)).start()

                @pl.when(to == me)
                def _():
                    mine[...] = piece

    def arrive(t):
        for k in range(steps):
            @pl.when(t == k)
            def _():
                for off in range(1, pg_n):
                    mode_in(off, k).wait_recv()

        @pl.when(jnp.logical_and(t == steps - 1, gets_x))
        def _():
            for p in range(pg_n):
                x_in(p).wait_recv()

        grads(t)

    whole = chunks - 1
    later = list(range(1, steps))

    arrive(0)
    pass_row()

    def open_two(i, carry):
        made = [tensor([0], chunk_of(chunks * i + k), (0, 1)) for k in range(chunks)]
        for k in range(chunks):
            for h in range(2):
                acc[chunks * i + k, h] = made[k][h]
        return carry

    lax.fori_loop(0, 1, open_two, 0)
    row_known()

    def arrive_later(t, carry):
        arrive(t)
        return carry

    lax.fori_loop(1, steps, arrive_later, 0)

    def finish(n, carry):
        made = tensor(later, chunk_of(n), (0, 1))
        for h in range(2):
            acc[n, h] += made[h]
        sib_copy(n).start()

        @pl.when(n == 0)
        def _():
            all_known()

        @pl.when(n > 0)
        def _():
            give(n - 1)
        return carry

    lax.fori_loop(0, whole, finish, 0)

    def finish_half(h, carry):
        acc[whole, h] += tensor(later, chunk_of(whole), (h,))[0]

        @pl.when(h == 0)
        def _():
            sib_copy(whole).start()
            give(whole - 1)
        return carry

    lax.fori_loop(0, 2, finish_half, 0)
    give(whole)

    for t in range(steps):
        for off in range(1, pg_n):
            mode_out(off, t).wait_send()
    for side, sends, _ in y_sides:
        @pl.when(sends)
        def _():
            for d in range(pg_n):
                y_out(side, d).wait_send()
    for side, sends in x_sides:
        @pl.when(sends)
        def _():
            for h in range(pg_n // 2):
                x_out(side, h).wait_send()
    for n in range(chunks):
        sib_copy(n).wait_send()
    for off in range(1, group_n):
        part_copy(off).wait()
    result = mine[...]
    for off in range(1, group_n):
        result = result + parts[lax.rem(me + off, group_n)].astype(F32)
    out_ref[...] = result


def shards(direct_modes, adjoint_modes, block_order):
    tx_n, ty_n, pg_n = lax.axis_size("tx"), lax.axis_size("ty"), lax.axis_size("pg")
    own_n, _, nx, lanes = direct_modes.shape
    adj_n = adjoint_modes.shape[0]
    mode_n = own_n * pg_n
    weight = 1.0 / math.sqrt(3.0 * nx * tx_n * lanes * ty_n)
    j_width, k_width = mode_n // ty_n, adj_n // tx_n
    blk = mode_n // NBLK
    half, width = nx // 2, j_width * own_n
    chunks = pg_n
    vmem = pl.BlockSpec(memory_space=pltpu.VMEM)
    dma = pltpu.SemaphoreType.DMA
    summed = pl.pallas_call(
        functools.partial(kernel, tx_n, ty_n, pg_n, weight),
        out_shape=jax.ShapeDtypeStruct((k_width, width), F32),
        in_specs=[pl.BlockSpec(memory_space=pltpu.SMEM)] + [pl.BlockSpec(memory_space=pl.ANY)] * 2,
        out_specs=vmem,
        scratch_shapes=[
            pltpu.VMEM((own_n, 3, nx, lanes), BF16),
            dma,
            pltpu.VMEM((nx * 3 * own_n, lanes), F32),
            pltpu.VMEM((nx, 3, own_n, lanes), BF16),
            pltpu.VMEM((adj_n, 3, nx, lanes), BF16),
            pltpu.VMEM((3 * half * adj_n, lanes), F32),
            dma,
            pltpu.VMEM((half + 2, pg_n, 3, own_n, lanes), BF16),
            pltpu.VMEM((2, 2, own_n, lanes), BF16),
            pltpu.VMEM((2, pg_n, own_n, lanes), BF16),
            pltpu.VMEM((half, 3, NBLK, blk, lanes), F32),
            pltpu.VMEM((half, 9, NBLK, blk, lanes), F32),
            pltpu.VMEM((half, 3, 2, own_n, lanes), WORK),
            pltpu.VMEM((half, 9, 2, own_n, lanes), WORK),
            pltpu.VMEM((chunks, 2, adj_n, own_n * own_n), F32),
            pltpu.VMEM((chunks, adj_n, own_n * own_n), F32),
            pltpu.VMEM((ty_n, tx_n, k_width, width), BF16),
            pltpu.VMEM((tx_n * ty_n, k_width, width), BF16),
            pltpu.VMEM((k_width, width), F32),
            dma((pg_n, half // 2)), dma((pg_n, half // 2)),
            dma((2, pg_n // 2)), dma((pg_n,)),
            dma((2, pg_n)), dma((2, pg_n)),
            dma((chunks,)), dma((chunks,)),
            dma((tx_n * ty_n,)), dma((tx_n * ty_n,)),
            pltpu.SemaphoreType.REGULAR((2,)), pltpu.SemaphoreType.REGULAR((2,)),
        ],
        compiler_params=pltpu.CompilerParams(
            collective_id=0, has_side_effects=True, vmem_limit_bytes=60 * 2**20),
    )(block_order, direct_modes, adjoint_modes)
    return jnp.transpose(summed.reshape(k_width, j_width, own_n), (2, 1, 0))


def solution(mesh):
    placed = (P("pg", None, "tx", "ty"), P(None, None, "tx", "ty"), P())
    return jax.shard_map(
        shards, mesh=mesh, in_specs=placed, out_specs=P("pg", "ty", "tx"), check_vma=False
    )
```
